32 devices in a mesh: dp: 4 (over y, x), ctx: 8 (over z, core).
Axes of the slice: x: 2, y: 2, z: 4, core: 2. Of those that a mesh axis runs over, the one named last changes fastest.
Arguments:
- inputs: float32 [4, 1024, 1088], P('dp', 'ctx'), may hold values from -6 to 6
- out_grad: float32 [4, 1024, 1088], P('dp', 'ctx'), may hold values from -6 to 6
- pair_blocks: int32 [8, 2], replicated, may hold values from 0 to 15, as said below
- triple_weight: float32 [1088, 3264], P('ctx', 'dp')
- merge_weight: float32 [1088, 1088], P('ctx', 'dp'), may hold values from -0.75 to 0.75
- expand_weight: float32 [1088, 4352], P('ctx', 'dp'), may hold values from -0.1875 to 0.1875
- shrink_weight: float32 [4352, 1088], P('ctx', 'dp'), may hold values from -0.09375 to 0.09375
- vector_params: float32 [1088, 12], P('ctx', 'dp')
- triple_moment: float32 [1088, 3264], P('ctx', 'dp'), may hold values from -24 to 24
- merge_moment: float32 [1088, 1088], P('ctx', 'dp'), may hold values from -6 to 6
- expand_moment: float32 [1088, 4352], P('ctx', 'dp'), may hold values from -6 to 6
- shrink_moment: float32 [4352, 1088], P('ctx', 'dp'), may hold values from -6 to 6
- vector_moment: float32 [1088, 12], P('ctx', 'dp'), may hold values from -112 to 112
- triple_square: float32 [1088, 3264], P('ctx', 'dp'), may hold values from 24.576 to 245.76
- merge_square: float32 [1088, 1088], P('ctx', 'dp'), may hold values from 8.192 to 81.92
- expand_square: float32 [1088, 4352], P('ctx', 'dp'), may hold values from 8.192 to 81.92
- shrink_square: float32 [4352, 1088], P('ctx', 'dp'), may hold values from 8.192 to 81.92
- vector_square: float32 [1088, 12], P('ctx', 'dp'), may hold values from 204.8 to 2048
Outputs:
- block_output: float32 [4, 1024, 1088], P('dp', 'ctx')
- input_grad: float32 [4, 1024, 1088], P('dp', 'ctx')
- triple_grad: float32 [1088, 3264], P('ctx', 'dp')
- merge_grad: float32 [1088, 1088], P('ctx', 'dp')
- expand_grad: float32 [1088, 4352], P('ctx', 'dp')
- shrink_grad: float32 [4352, 1088], P('ctx', 'dp')
- vector_grad: float32 [1088, 12], P('ctx', 'dp')
- triple_new: float32 [1088, 3264], P('ctx', 'dp')
- merge_new: float32 [1088, 1088], P('ctx', 'dp')
- expand_new: float32 [1088, 4352], P('ctx', 'dp')
- shrink_new: float32 [4352, 1088], P('ctx', 'dp')
- vector_new: float32 [1088, 12], P('ctx', 'dp')
- triple_moment_new: float32 [1088, 3264], P('ctx', 'dp')
- merge_moment_new: float32 [1088, 1088], P('ctx', 'dp')
- expand_moment_new: float32 [1088, 4352], P('ctx', 'dp')
- shrink_moment_new: float32 [4352, 1088], P('ctx', 'dp')
- vector_moment_new: float32 [1088, 12], P('ctx', 'dp')
- triple_square_new: float32 [1088, 3264], P('ctx', 'dp')
- merge_square_new: float32 [1088, 1088], P('ctx', 'dp')
- expand_square_new: float32 [1088, 4352], P('ctx', 'dp')
- shrink_square_new: float32 [4352, 1088], P('ctx', 'dp')
- vector_square_new: float32 [1088, 12], P('ctx', 'dp')
The draws below stay inside these ranges and needn't reach their ends.
Inputs may be any that keep to these rules, and one draw needn't show every extreme that they name: `pair_blocks`: row c names the two blocks of 64 positions that stand in stored rows c * 2 * 64 onward: first a block p, then 2 * 8 - 1 - p; each of the 16 blocks is named once.
All inputs are finite; a program needn't handle non-finite values.
Results may differ from the reference program's by a relative error of at most 0.011.
Values may be sent and summed in bfloat16 or wider, within the bound.
A program may use at most 256 MiB of HBM per device.

```python
import math
import jax
import jax.numpy as jnp
from jax import lax

D = 1088
H = 17
HD = 64
FF = 4352
BLK = 64
PAIRS = 8
SEQ = 1024
SEQS = 4
TOKENS = 4096


def draw_pair_blocks(key, part):
    order = jax.random.permutation(key, PAIRS).astype(jnp.int32)
    return jnp.stack([order, 2 * PAIRS - 1 - order], axis=1).astype(jnp.int32)


def draw_triple_weight(key, part):
    return jax.random.normal(key, (D, 3 * D), jnp.float32) * D ** (-0.5)


def draw_vector_params(key, part):
    noise = jax.random.normal(key, (D, 12), jnp.float32) * 0.2
    columns = jnp.arange(12, dtype=jnp.int32)
    offset = jnp.where((columns == 0) | (columns == 5), 1.0, 0.0).astype(jnp.float32)
    return noise + offset[None, :]


def levels(rng, dims, split, low, high):
    def one(axis_at, shards_of):
        steps = jax.random.uniform(jax.random.fold_in(jax.random.fold_in(rng, 6), axis_at), (shards_of,), jnp.float32, low / len(split), high / len(split))
        return jnp.repeat(jnp.exp(steps), dims[axis_at] // shards_of).reshape((-1,) + (1,) * (len(dims) - axis_at - 1))

    loudness = one(*split[0])
    for cut in split[1:]:
        loudness = loudness * one(*cut)
    return loudness


def centred(own_key, extent, deviation, reach, cuts=(), kind=jnp.bfloat16):
    entries = jax.random.normal(own_key, extent, jnp.float32) * deviation
    if len(cuts) > 0:
        entries = levels(own_key, extent, cuts, -0.22, 0.18) * entries
    return jnp.clip(entries, min=-reach, max=reach).astype(kind)


def setup_inputs(seed: int = 0) -> dict:
    keys = jax.random.split(jax.random.key(seed), 19)
    return {
        "inputs": centred(keys[0], (SEQS, SEQ, D), 1.0, 6.0, ((0, 4), (1, 8)), jnp.float32),
        "out_grad": centred(keys[1], (SEQS, SEQ, D), 1.0, 6.0, ((0, 4), (1, 8)), jnp.float32),
        "pair_blocks": draw_pair_blocks(jax.random.fold_in(keys[18], 71), 0),
        "triple_weight": draw_triple_weight(jax.random.fold_in(keys[18], 71), 0),
        "merge_weight": centred(keys[4], (D, D), (max(1, D * 64 // SEQ)) ** -0.5, 0.75, ((0, 8), (1, 4)), jnp.float32),
        "expand_weight": centred(keys[5], (D, FF), D ** -0.5, 0.1875, ((0, 8), (1, 4)), jnp.float32),
        "shrink_weight": centred(keys[6], (FF, D), FF ** -0.5, 0.09375, ((0, 8), (1, 4)), jnp.float32),
        "vector_params": draw_vector_params(jax.random.fold_in(keys[18], 71), 0),
        "triple_moment": centred(keys[8], (D, 3 * D), (0.06 * TOKENS ** 0.5), 24.0, ((0, 8), (1, 4)), jnp.float32),
        "merge_moment": centred(keys[9], (D, D), (0.03 * TOKENS ** 0.5), 6.0, ((0, 8), (1, 4)), jnp.float32),
        "expand_moment": centred(keys[10], (D, FF), (0.03 * TOKENS ** 0.5), 6.0, ((0, 8), (1, 4)), jnp.float32),
        "shrink_moment": centred(keys[11], (FF, D), (0.03 * TOKENS ** 0.5), 6.0, ((0, 8), (1, 4)), jnp.float32),
        "vector_moment": centred(keys[12], (D, 12), (0.3 * TOKENS ** 0.5), 112.0, ((0, 8), (1, 4)), jnp.float32),
        "triple_square": jnp.clip(jnp.exp(math.log(245.76) - 2.3025851 * jax.random.uniform(keys[13], (D, 3 * D), jnp.float32) ** levels(keys[13], (D, 3 * D), ((0, 8), (1, 4)), -0.2, 0.2)), 24.576, 245.76),
        "merge_square": jnp.clip(jnp.exp(math.log(81.92) - 2.30258502 * jax.random.uniform(keys[14], (D, D), jnp.float32) ** levels(keys[14], (D, D), ((0, 8), (1, 4)), -0.2, 0.2)), 8.192, 81.92),
        "expand_square": jnp.clip(jnp.exp(math.log(81.92) - 2.30258502 * jax.random.uniform(keys[15], (D, FF), jnp.float32) ** levels(keys[15], (D, FF), ((0, 8), (1, 4)), -0.2, 0.2)), 8.192, 81.92),
        "shrink_square": jnp.clip(jnp.exp(math.log(81.92) - 2.30258502 * jax.random.uniform(keys[16], (FF, D), jnp.float32) ** levels(keys[16], (FF, D), ((0, 8), (1, 4)), -0.2, 0.2)), 8.192, 81.92),
        "vector_square": jnp.clip(jnp.exp(math.log(2048.0) - 2.3025851 * jax.random.uniform(keys[17], (D, 12), jnp.float32) ** levels(keys[17], (D, 12), ((0, 8), (1, 4)), -0.2, 0.2)), 204.8, 2048.0),
    }


norm_eps = 1e-05
beta_first = 0.9
beta_second = 0.95
learn_rate = 0.01
decay_rate = 0.1
adam_eps = 1e-08
adam_steps = 4
gelu_coef = 0.7978845608028654
masked_score = -1e+30

def layer_norm(values):
    center = lax.optimization_barrier(jnp.mean(values, axis=-1, keepdims=True))
    shifted = values - center
    inverse = lax.rsqrt(lax.optimization_barrier(jnp.mean(shifted * shifted, axis=-1, keepdims=True)) + norm_eps)
    return (shifted * inverse, inverse)

def norm_back(incoming, normed, inverse, gain_vec):
    scaled = incoming * gain_vec
    return inverse * (scaled - lax.optimization_barrier(jnp.mean(scaled, axis=-1, keepdims=True)) - normed * lax.optimization_barrier(jnp.mean(scaled * normed, axis=-1, keepdims=True)))

def gelu_value(values):
    inside = gelu_coef * (values + 0.044715 * values * values * values)
    return 0.5 * values * (1.0 + jnp.tanh(inside))

def gelu_slope(values):
    inside = gelu_coef * (values + 0.044715 * values * values * values)
    tangent = jnp.tanh(inside)
    return 0.5 * (1.0 + tangent) + 0.5 * values * (1.0 - tangent * tangent) * gelu_coef * (1.0 + 3.0 * 0.044715 * values * values)

def adam_update(weight, gradient, moment, square, decayed):
    moment_new = beta_first * moment + (1.0 - beta_first) * gradient
    square_new = beta_second * square + (1.0 - beta_second) * gradient * gradient
    first_fix = 1.0 - beta_first ** adam_steps
    second_fix = 1.0 - beta_second ** adam_steps
    direction = moment_new / first_fix / (jnp.sqrt(square_new / second_fix) + adam_eps)
    if decayed:
        direction = direction + decay_rate * weight
    return (weight - learn_rate * direction, moment_new, square_new)

def attend_forward(query_b, key_b, value_b, positions):
    block_rows = min(512, SEQ)
    keys_full = key_b.astype(jnp.float32).reshape(SEQ, H, HD)
    values_full = value_b.astype(jnp.float32).reshape(SEQ, H, HD)
    score_scale = HD ** (-0.5)

    def one_block(index):
        start = index * block_rows
        query_full = lax.dynamic_slice_in_dim(query_b, start, block_rows, 0).astype(jnp.float32).reshape(block_rows, H, HD)
        query_pos = lax.dynamic_slice_in_dim(positions, start, block_rows, 0)
        scores = jnp.einsum('qhd,khd->hqk', query_full, keys_full) * score_scale
        allowed = query_pos[:, None] >= positions[None, :]
        scores = jnp.where(allowed[None, :, :], scores, masked_score)
        row_max = lax.optimization_barrier(jnp.max(scores, axis=2, keepdims=True))
        log_total = row_max + jnp.log(lax.optimization_barrier(jnp.sum(jnp.exp(scores - row_max), axis=2, keepdims=True)))
        probs_b = jnp.exp(scores - log_total).astype(jnp.bfloat16)
        attended = jnp.einsum('hqk,khd->qhd', probs_b.astype(jnp.float32), values_full)
        return (attended.reshape(block_rows, D).astype(jnp.bfloat16), log_total[:, :, 0])
    blocks_out, log_totals = lax.map(one_block, jnp.arange(SEQ // block_rows, dtype=jnp.int32))
    return (blocks_out.reshape(SEQ, D), log_totals)

def attend_backward(query_b, key_b, value_b, attended_b, dattended_b, log_totals, positions):
    block_rows = min(512, SEQ)
    keys_full = key_b.astype(jnp.float32).reshape(SEQ, H, HD)
    values_full = value_b.astype(jnp.float32).reshape(SEQ, H, HD)
    score_scale = HD ** (-0.5)

    def one_block(carry, inputs_block):
        dkey_sum, dvalue_sum = carry
        index, log_total = inputs_block
        start = index * block_rows
        query_full = lax.dynamic_slice_in_dim(query_b, start, block_rows, 0).astype(jnp.float32).reshape(block_rows, H, HD)
        dout_full = lax.dynamic_slice_in_dim(dattended_b, start, block_rows, 0).astype(jnp.float32).reshape(block_rows, H, HD)
        out_full = lax.dynamic_slice_in_dim(attended_b, start, block_rows, 0).astype(jnp.float32).reshape(block_rows, H, HD)
        query_pos = lax.dynamic_slice_in_dim(positions, start, block_rows, 0)
        scores = jnp.einsum('qhd,khd->hqk', query_full, keys_full) * score_scale
        allowed = query_pos[:, None] >= positions[None, :]
        scores = jnp.where(allowed[None, :, :], scores, masked_score)
        probs = jnp.exp(scores - log_total[:, :, None])
        probs_b = probs.astype(jnp.bfloat16)
        delta = lax.optimization_barrier(jnp.sum(dout_full * out_full, axis=2)).transpose(1, 0)[:, :, None]
        dprobs = jnp.einsum('qhd,khd->hqk', dout_full, values_full)
        dscores_b = (probs * (dprobs - delta) * score_scale).astype(jnp.bfloat16)
        dscores_full = dscores_b.astype(jnp.float32)
        dquery = jnp.einsum('hqk,khd->qhd', dscores_full, keys_full).reshape(block_rows, D)
        dkey_sum = dkey_sum + jnp.einsum('hqk,qhd->khd', dscores_full, query_full)
        dvalue_sum = dvalue_sum + jnp.einsum('hqk,qhd->khd', probs_b.astype(jnp.float32), dout_full)
        return ((dkey_sum, dvalue_sum), dquery)
    empty = jnp.zeros((SEQ, H, HD), jnp.float32)
    indices = jnp.arange(SEQ // block_rows, dtype=jnp.int32)
    (dkey_sum, dvalue_sum), dquery_blocks = lax.scan(one_block, (empty, empty), (indices, log_totals))
    return (dquery_blocks.reshape(SEQ, D), dkey_sum.reshape(SEQ, D), dvalue_sum.reshape(SEQ, D))

def one_sequence(stream, cotangent, positions, copies):
    w_triple, w_merge, w_expand, w_shrink, w_vector = copies
    vectors = w_vector.astype(jnp.float32)
    gain_one = vectors[:, 0]
    shift_one = vectors[:, 1]
    query_bias = vectors[:, 2]
    value_bias = vectors[:, 3]
    merge_bias = vectors[:, 4]
    gain_two = vectors[:, 5]
    shift_two = vectors[:, 6]
    shrink_bias = vectors[:, 7]
    expand_bias = vectors[:, 8:12].T.reshape(-1)
    normed_one, inverse_one = layer_norm(stream)
    act_one = (normed_one * gain_one + shift_one).astype(jnp.bfloat16)
    triple = jnp.dot(act_one, w_triple, preferred_element_type=jnp.float32)
    query_b = (triple[:, :D] + query_bias).astype(jnp.bfloat16)
    key_b = triple[:, D:2 * D].astype(jnp.bfloat16)
    value_b = (triple[:, 2 * D:] + value_bias).astype(jnp.bfloat16)
    attended_b, log_totals = attend_forward(query_b, key_b, value_b, positions)
    middle = stream + jnp.dot(attended_b, w_merge, preferred_element_type=jnp.float32) + merge_bias
    normed_two, inverse_two = layer_norm(middle)
    act_two = (normed_two * gain_two + shift_two).astype(jnp.bfloat16)
    pre_act = jnp.dot(act_two, w_expand, preferred_element_type=jnp.float32) + expand_bias
    hidden_b = gelu_value(pre_act).astype(jnp.bfloat16)
    block_out = middle + jnp.dot(hidden_b, w_shrink, preferred_element_type=jnp.float32) + shrink_bias
    cotangent_b = cotangent.astype(jnp.bfloat16)
    shrink_local = jnp.dot(hidden_b.T, cotangent_b, preferred_element_type=jnp.float32)
    shrink_bias_grad = lax.optimization_barrier(jnp.sum(cotangent, axis=0))
    dpre = jnp.dot(cotangent_b, w_shrink.T, preferred_element_type=jnp.float32) * gelu_slope(pre_act)
    dpre_b = dpre.astype(jnp.bfloat16)
    expand_local = jnp.dot(act_two.T, dpre_b, preferred_element_type=jnp.float32)
    expand_bias_grad = lax.optimization_barrier(jnp.sum(dpre, axis=0))
    dact_two = jnp.dot(dpre_b, w_expand.T, preferred_element_type=jnp.float32)
    gain_two_grad = lax.optimization_barrier(jnp.sum(dact_two * normed_two, axis=0))
    shift_two_grad = lax.optimization_barrier(jnp.sum(dact_two, axis=0))
    dmiddle = cotangent + norm_back(dact_two, normed_two, inverse_two, gain_two)
    dmiddle_b = dmiddle.astype(jnp.bfloat16)
    merge_local = jnp.dot(attended_b.T, dmiddle_b, preferred_element_type=jnp.float32)
    merge_bias_grad = lax.optimization_barrier(jnp.sum(dmiddle, axis=0))
    dattended_b = jnp.dot(dmiddle_b, w_merge.T, preferred_element_type=jnp.float32).astype(jnp.bfloat16)
    dquery, dkey, dvalue = attend_backward(query_b, key_b, value_b, attended_b, dattended_b, log_totals, positions)
    dtriple_b = jnp.concatenate([dquery, dkey, dvalue], axis=1).astype(jnp.bfloat16)
    triple_local = jnp.dot(act_one.T, dtriple_b, preferred_element_type=jnp.float32)
    query_bias_grad = lax.optimization_barrier(jnp.sum(dquery, axis=0))
    value_bias_grad = lax.optimization_barrier(jnp.sum(dvalue, axis=0))
    dact_one = jnp.dot(dtriple_b, w_triple.T, preferred_element_type=jnp.float32)
    gain_one_grad = lax.optimization_barrier(jnp.sum(dact_one * normed_one, axis=0))
    shift_one_grad = lax.optimization_barrier(jnp.sum(dact_one, axis=0))
    input_rows = dmiddle + norm_back(dact_one, normed_one, inverse_one, gain_one)
    vector_local = jnp.concatenate([jnp.stack([gain_one_grad, shift_one_grad, query_bias_grad, value_bias_grad, merge_bias_grad, gain_two_grad, shift_two_grad, shrink_bias_grad], axis=1), expand_bias_grad.reshape(4, D).T], axis=1)
    return (block_out, input_rows, (triple_local, merge_local, expand_local, shrink_local, vector_local))

def reference(inputs, out_grad, pair_blocks, triple_weight, merge_weight, expand_weight, shrink_weight, vector_params, triple_moment, merge_moment, expand_moment, shrink_moment, vector_moment, triple_square, merge_square, expand_square, shrink_square, vector_square):
    offsets = jnp.arange(BLK, dtype=jnp.int32)
    positions = (pair_blocks.reshape(-1)[:, None] * BLK + offsets[None, :]).reshape(-1).astype(jnp.int32)
    masters = (triple_weight, merge_weight, expand_weight, shrink_weight, vector_params)
    copies = tuple((master.astype(jnp.bfloat16) for master in masters))

    def per_sequence(totals, sequence_pair):
        stream, cotangent = sequence_pair
        block_out, input_rows, grads = one_sequence(stream, cotangent, positions, copies)
        return (tuple((running + grad_part for running, grad_part in zip(totals, grads))), (block_out, input_rows))
    zeros = tuple((jnp.zeros(master.shape, jnp.float32) for master in masters))
    totals, (block_output, input_grad) = lax.scan(per_sequence, zeros, (inputs, out_grad))
    moments = (triple_moment, merge_moment, expand_moment, shrink_moment, vector_moment)
    squares = (triple_square, merge_square, expand_square, shrink_square, vector_square)
    updated = [adam_update(masters[number], totals[number], moments[number], squares[number], number < 4) for number in range(5)]
    return (block_output, input_grad, totals[0], totals[1], totals[2], totals[3], totals[4], updated[0][0], updated[1][0], updated[2][0], updated[3][0], updated[4][0], updated[0][1], updated[1][1], updated[2][1], updated[3][1], updated[4][1], updated[0][2], updated[1][2], updated[2][2], updated[3][2], updated[4][2])
```

```python
import jax
import jax.numpy as jnp
from jax import lax
from jax.experimental import pallas as pl
from jax.experimental.pallas import tpu as pltpu
from jax.sharding import PartitionSpec as P

D = 1088
H = 17
HD = 64
BLK = 64


norm_eps = 1e-05
beta_first = 0.9
beta_second = 0.95
learn_rate = 0.01
decay_rate = 0.1
adam_eps = 1e-08
adam_steps = 4
gelu_coef = 0.7978845608028654
masked_score = -1e30


def layer_norm(values):
    center = jnp.mean(values, axis=-1, keepdims=True)
    shifted = values - center
    inverse = lax.rsqrt(jnp.mean(shifted * shifted, axis=-1, keepdims=True) + norm_eps)
    return (shifted * inverse, inverse)


def norm_back(incoming, normed, inverse, gain_vec):
    scaled = incoming * gain_vec
    return inverse * (
        scaled
        - jnp.mean(scaled, axis=-1, keepdims=True)
        - normed * jnp.mean(scaled * normed, axis=-1, keepdims=True)
    )


def gelu_value(values):
    inside = gelu_coef * (values + 0.044715 * values * values * values)
    return 0.5 * values * (1.0 + jnp.tanh(inside))


def gelu_slope(values):
    inside = gelu_coef * (values + 0.044715 * values * values * values)
    tangent = jnp.tanh(inside)
    return 0.5 * (1.0 + tangent) + 0.5 * values * (1.0 - tangent * tangent) * gelu_coef * (
        1.0 + 3.0 * 0.044715 * values * values
    )


def adam_update(weight, gradient, moment, square, decayed):
    moment_new = beta_first * moment + (1.0 - beta_first) * gradient
    square_new = beta_second * square + (1.0 - beta_second) * gradient * gradient
    first_fix = 1.0 - beta_first**adam_steps
    second_fix = 1.0 - beta_second**adam_steps
    direction = moment_new / first_fix / (jnp.sqrt(square_new / second_fix) + adam_eps)
    if decayed:
        direction = direction + decay_rate * weight
    return (weight - learn_rate * direction, moment_new, square_new)


def dot_on(left, right, left_dim, right_dim):
    return lax.dot_general(
        left, right, (((left_dim,), (right_dim,)), ((), ())), preferred_element_type=jnp.float32
    )


def head_probs(query_t, key_t, allowed):
    scores = dot_on(query_t, key_t, 0, 0) * HD ** (-0.5)
    scores = jnp.where(allowed, scores, masked_score)
    row_max = jnp.max(scores, axis=1, keepdims=True)
    weights = jnp.exp(scores - row_max)
    return weights / jnp.sum(weights, axis=1, keepdims=True)


def forward_kernel(query_pos, key_pos, query_ref, key_ref, value_ref, out_ref):
    allowed = query_pos[...] >= key_pos[...]
    probs = head_probs(query_ref[...], key_ref[...], allowed).astype(jnp.bfloat16)
    out_ref[...] = dot_on(value_ref[...], probs, 1, 1).astype(jnp.bfloat16)


def backward_kernel(
    query_pos, key_pos, query_ref, key_ref, value_ref, out_ref, dout_ref, dquery, dkey, dvalue
):
    allowed = query_pos[...] >= key_pos[...]
    query_t = query_ref[...]
    key_t = key_ref[...]
    dout_t = dout_ref[...]
    probs = head_probs(query_t, key_t, allowed)
    dprobs = dot_on(dout_t, value_ref[...], 0, 0)
    products = dout_t.astype(jnp.float32) * out_ref[...].astype(jnp.float32)
    delta = jnp.sum(products.T, axis=1, keepdims=True)
    dscores = (probs * (dprobs - delta) * HD ** (-0.5)).astype(jnp.bfloat16)
    dquery[...] = dot_on(key_t, dscores, 1, 1).astype(jnp.bfloat16)
    dkey[...] = dot_on(query_t, dscores, 1, 0).astype(jnp.bfloat16)
    dvalue[...] = dot_on(dout_t, probs.astype(jnp.bfloat16), 1, 0).astype(jnp.bfloat16)


def attention(kernel, query_pos, key_pos, features, out_rows):
    queries, keys = query_pos.shape[0], key_pos.shape[1]
    whole = lambda array: pl.BlockSpec(array.shape, lambda h: (0, 0))
    block = lambda width: pl.BlockSpec((HD, width), lambda h: (h, 0))
    shapes = [jax.ShapeDtypeStruct((H * HD, width), jnp.bfloat16) for width in out_rows]
    flops = 2 * H * HD * queries * keys * (2 if len(out_rows) == 1 else 5)
    return pl.pallas_call(
        kernel,
        grid=(H,),
        in_specs=[whole(query_pos), whole(key_pos)] + [block(x.shape[1]) for x in features],
        out_specs=[block(width) for width in out_rows],
        out_shape=shapes,
        cost_estimate=pl.CostEstimate(
            flops=flops, bytes_accessed=8 * H * HD * keys, transcendentals=H * queries * keys
        ),
    )(query_pos, key_pos, *features)


def exchange(blocks):
    return lax.all_to_all(blocks, "ctx", split_axis=0, concat_axis=0, tiled=True)


def scatter_rows(partial):
    return lax.psum_scatter(
        partial.astype(jnp.bfloat16), "ctx", scatter_dimension=0, tiled=True
    ).astype(jnp.float32)


def gather_rows(rows):
    return lax.all_gather(rows, "ctx", axis=0, tiled=True)


def local(
    inputs,
    out_grad,
    pair_blocks,
    triple_weight,
    merge_weight,
    expand_weight,
    shrink_weight,
    vector_params,
    triple_moment,
    merge_moment,
    expand_moment,
    shrink_moment,
    vector_moment,
    triple_square,
    merge_square,
    expand_square,
    shrink_square,
    vector_square,
):
    bf16 = jnp.bfloat16
    n = lax.axis_size("ctx")
    m = lax.axis_size("dp")
    here = lax.axis_index("ctx")
    rows = inputs.shape[1]
    total = rows * n
    feat = D // n
    hidden_width = m * expand_weight.shape[1]
    wide = hidden_width // n
    stream = inputs[0]
    cotangent = out_grad[0]
    offsets = jnp.arange(BLK, dtype=jnp.int32)
    positions = (pair_blocks.reshape(-1)[:, None] * BLK + offsets[None, :]).reshape(-1)
    query_pos = lax.dynamic_slice_in_dim(positions, here * rows, rows)[:, None]
    key_pos = positions[None, :]

    packed = jnp.concatenate(
        [
            triple_weight.astype(bf16),
            merge_weight.astype(bf16),
            expand_weight.astype(bf16),
            vector_params.astype(bf16),
        ],
        axis=1,
    )
    tw, mw, ew = triple_weight.shape[1], merge_weight.shape[1], expand_weight.shape[1]
    columns = lax.all_gather(packed, "dp", axis=0)

    def take(start, width):
        return columns[:, :, start : start + width].transpose(1, 0, 2).reshape(feat, m * width)

    triple_rows = take(0, tw)
    merge_rows = take(tw, mw)
    expand_rows = take(tw + mw, ew)
    vector_rows = take(tw + mw + ew, vector_params.shape[1])
    normed_one, inverse_one = layer_norm(stream)
    normed_full = gather_rows(normed_one.astype(bf16))
    send = jnp.concatenate(
        [
            triple_rows.reshape(feat, 3, n, feat).transpose(2, 0, 1, 3).reshape(n, feat, 3 * feat),
            expand_rows.reshape(feat, n, wide).transpose(1, 0, 2),
        ],
        axis=2,
    )
    got = exchange(send).reshape(D, 3 * feat + wide)
    w_triple = got[:, : 3 * feat]
    w_expand = got[:, 3 * feat :]
    merged = gather_rows(jnp.concatenate([merge_rows, vector_rows], axis=1))
    w_merge = merged[:, :D]
    vectors = merged[:, D:].astype(jnp.float32)
    gain_one = vectors[:, 0]
    shift_one = vectors[:, 1]
    query_bias = lax.dynamic_slice_in_dim(vectors[:, 2], here * feat, feat)
    value_bias = lax.dynamic_slice_in_dim(vectors[:, 3], here * feat, feat)
    merge_bias = vectors[:, 4]
    gain_two = vectors[:, 5]
    shift_two = vectors[:, 6]
    shrink_bias = vectors[:, 7]
    expand_bias = lax.dynamic_slice_in_dim(vectors[:, 8:].T.reshape(-1), here * wide, wide)

    act_one = (normed_full.astype(jnp.float32) * gain_one + shift_one).astype(bf16)
    bias = jnp.concatenate([query_bias, jnp.zeros_like(query_bias), value_bias])
    triple_t = (dot_on(w_triple, act_one, 0, 1) + bias[:, None]).astype(bf16)
    query_t = exchange(triple_t[:feat].reshape(feat, n, rows).transpose(1, 0, 2)).reshape(D, rows)
    both = lax.all_gather(triple_t[feat:].reshape(2, feat, total), "ctx", axis=0)
    key_t = both[:, 0].reshape(D, total)
    value_t = both[:, 1].reshape(D, total)
    (attended_t,) = attention(
        forward_kernel, query_pos, key_pos, (query_t, key_t, value_t), (rows,)
    )
    cot_full = gather_rows(cotangent.astype(bf16))
    w_shrink = (
        lax.all_gather(shrink_weight.astype(bf16), "dp", axis=0).transpose(1, 0, 2).reshape(wide, D)
    )
    middle = stream + dot_on(attended_t, w_merge, 0, 0) + merge_bias
    normed_two, inverse_two = layer_norm(middle)
    act_two = gather_rows((normed_two * gain_two + shift_two).astype(bf16))
    pre_act = dot_on(act_two, w_expand, 1, 0) + expand_bias
    hidden_b = gelu_value(pre_act).astype(bf16)
    dpre = dot_on(cot_full, w_shrink, 1, 1) * gelu_slope(pre_act)
    dpre_b = dpre.astype(bf16)
    expand_bias_grad = jnp.sum(dpre, axis=0)
    dact_two = scatter_rows(dot_on(dpre_b, w_expand, 1, 1))
    block_out = middle + scatter_rows(dot_on(hidden_b, w_shrink, 1, 0)) + shrink_bias
    shrink_part = dot_on(hidden_b, cot_full, 0, 0).astype(bf16)
    expand_part = dot_on(act_two, dpre_b, 0, 0).astype(bf16)
    shrink_grad = lax.psum_scatter(
        shrink_part.reshape(wide, m, D // m).transpose(1, 0, 2), "dp", scatter_dimension=0
    ).astype(jnp.float32)
    shrink_bias_grad = jnp.sum(cotangent, axis=0)
    gain_two_grad = jnp.sum(dact_two * normed_two, axis=0)
    shift_two_grad = jnp.sum(dact_two, axis=0)
    dmiddle = cotangent + norm_back(dact_two, normed_two, inverse_two, gain_two)
    dmiddle_b = dmiddle.astype(bf16)
    merge_part = lax.psum_scatter(
        dot_on(attended_t, dmiddle_b, 1, 0).astype(bf16), "ctx", scatter_dimension=0, tiled=True
    )
    merge_bias_grad = jnp.sum(dmiddle, axis=0)
    dattended_t = dot_on(w_merge, dmiddle_b, 1, 1).astype(bf16)
    dquery_t, dkey_t, dvalue_t = attention(
        backward_kernel,
        query_pos,
        key_pos,
        (query_t, key_t, value_t, attended_t, dattended_t),
        (rows, total, total),
    )
    dquery_c = exchange(dquery_t.reshape(n, feat, rows)).transpose(1, 0, 2).reshape(feat, total)
    dkey_c = lax.psum_scatter(dkey_t, "ctx", scatter_dimension=0, tiled=True)
    dvalue_c = lax.psum_scatter(dvalue_t, "ctx", scatter_dimension=0, tiled=True)
    dtriple_t = jnp.concatenate([dquery_c, dkey_c, dvalue_c], axis=0)
    query_bias_grad = jnp.sum(dquery_c.astype(jnp.float32), axis=1)
    value_bias_grad = jnp.sum(dvalue_c.astype(jnp.float32), axis=1)
    dact_one = scatter_rows(dot_on(dtriple_t, w_triple, 0, 1))
    triple_part = dot_on(act_one, dtriple_t, 0, 1).astype(bf16)
    gain_one_grad = jnp.sum(dact_one * normed_one, axis=0)
    shift_one_grad = jnp.sum(dact_one, axis=0)
    input_rows = dmiddle + norm_back(dact_one, normed_one, inverse_one, gain_one)

    def place(piece, size):
        return lax.dynamic_update_slice_in_dim(
            jnp.zeros((size,), jnp.float32), piece, here * piece.shape[0], 0
        )

    vector_local = jnp.concatenate(
        [
            jnp.stack(
                [
                    gain_one_grad,
                    shift_one_grad,
                    place(query_bias_grad, D),
                    place(value_bias_grad, D),
                    merge_bias_grad,
                    gain_two_grad,
                    shift_two_grad,
                    shrink_bias_grad,
                ],
                axis=1,
            ),
            place(expand_bias_grad, hidden_width).reshape(-1, D).T,
        ],
        axis=1,
    )
    vector_part = lax.psum_scatter(vector_local, "ctx", scatter_dimension=0, tiled=True)

    def by_dp(rows_part):
        return rows_part.reshape(feat, m, -1).transpose(1, 0, 2)

    expand_rows_part = exchange(expand_part.reshape(n, feat, wide)).transpose(1, 0, 2)
    expand_grad = lax.psum_scatter(by_dp(expand_rows_part), "dp", scatter_dimension=0).astype(
        jnp.float32
    )
    triple_rows_part = (
        exchange(triple_part.reshape(n, feat, 3 * feat))
        .reshape(n, feat, 3, feat)
        .transpose(1, 2, 0, 3)
    )
    last = lax.psum_scatter(
        jnp.concatenate(
            [by_dp(triple_rows_part), by_dp(merge_part), by_dp(vector_part).astype(bf16)], axis=2
        ),
        "dp",
        scatter_dimension=0,
    ).astype(jnp.float32)
    triple_grad = last[:, :tw]
    merge_grad = last[:, tw : tw + mw]
    vector_grad = last[:, tw + mw :]
    triple_new, triple_moment_new, triple_square_new = adam_update(
        triple_weight, triple_grad, triple_moment, triple_square, True
    )
    merge_new, merge_moment_new, merge_square_new = adam_update(
        merge_weight, merge_grad, merge_moment, merge_square, True
    )
    expand_new, expand_moment_new, expand_square_new = adam_update(
        expand_weight, expand_grad, expand_moment, expand_square, True
    )
    shrink_new, shrink_moment_new, shrink_square_new = adam_update(
        shrink_weight, shrink_grad, shrink_moment, shrink_square, True
    )
    vector_new, vector_moment_new, vector_square_new = adam_update(
        vector_params, vector_grad, vector_moment, vector_square, False
    )
    return (
        block_out[None],
        input_rows[None],
        triple_grad,
        merge_grad,
        expand_grad,
        shrink_grad,
        vector_grad,
        triple_new,
        merge_new,
        expand_new,
        shrink_new,
        vector_new,
        triple_moment_new,
        merge_moment_new,
        expand_moment_new,
        shrink_moment_new,
        vector_moment_new,
        triple_square_new,
        merge_square_new,
        expand_square_new,
        shrink_square_new,
        vector_square_new,
    )


def solution(mesh):
    in_specs = (
        P("dp", "ctx", None),
        P("dp", "ctx", None),
        P(),
        P("ctx", "dp"),
        P("ctx", "dp"),
        P("ctx", "dp"),
        P("ctx", "dp"),
        P("ctx", "dp"),
        P("ctx", "dp"),
        P("ctx", "dp"),
        P("ctx", "dp"),
        P("ctx", "dp"),
        P("ctx", "dp"),
        P("ctx", "dp"),
        P("ctx", "dp"),
        P("ctx", "dp"),
        P("ctx", "dp"),
        P("ctx", "dp"),
    )
    out_specs = (
        P("dp", "ctx", None),
        P("dp", "ctx", None),
        P("ctx", "dp"),
        P("ctx", "dp"),
        P("ctx", "dp"),
        P("ctx", "dp"),
        P("ctx", "dp"),
        P("ctx", "dp"),
        P("ctx", "dp"),
        P("ctx", "dp"),
        P("ctx", "dp"),
        P("ctx", "dp"),
        P("ctx", "dp"),
        P("ctx", "dp"),
        P("ctx", "dp"),
        P("ctx", "dp"),
        P("ctx", "dp"),
        P("ctx", "dp"),
        P("ctx", "dp"),
        P("ctx", "dp"),
        P("ctx", "dp"),
        P("ctx", "dp"),
    )
    return jax.shard_map(local, mesh=mesh, in_specs=in_specs, out_specs=out_specs, check_vma=False)
```

```python
import jax
import jax.numpy as jnp
from jax import lax
from jax.experimental import pallas as pl
from jax.experimental.pallas import tpu as pltpu
from jax.sharding import PartitionSpec as P

D = 1088
H = 17
HD = 64
BLK = 64


norm_eps = 1e-05
beta_first = 0.9
beta_second = 0.95
learn_rate = 0.01
decay_rate = 0.1
adam_eps = 1e-08
adam_steps = 4
gelu_coef = 0.7978845608028654
masked_score = -1e30


def layer_norm(values):
    center = jnp.mean(values, axis=-1, keepdims=True)
    shifted = values - center
    inverse = lax.rsqrt(jnp.mean(shifted * shifted, axis=-1, keepdims=True) + norm_eps)
    return (shifted * inverse, inverse)


def norm_back(incoming, normed, inverse, gain_vec):
    scaled = incoming * gain_vec
    return inverse * (
        scaled
        - jnp.mean(scaled, axis=-1, keepdims=True)
        - normed * jnp.mean(scaled * normed, axis=-1, keepdims=True)
    )


def gelu_value(values):
    inside = gelu_coef * (values + 0.044715 * values * values * values)
    return 0.5 * values * (1.0 + jnp.tanh(inside))


def gelu_slope(values):
    inside = gelu_coef * (values + 0.044715 * values * values * values)
    tangent = jnp.tanh(inside)
    return 0.5 * (1.0 + tangent) + 0.5 * values * (1.0 - tangent * tangent) * gelu_coef * (
        1.0 + 3.0 * 0.044715 * values * values
    )


def adam_update(weight, gradient, moment, square, decayed):
    moment_new = beta_first * moment + (1.0 - beta_first) * gradient
    square_new = beta_second * square + (1.0 - beta_second) * gradient * gradient
    first_fix = 1.0 - beta_first**adam_steps
    second_fix = 1.0 - beta_second**adam_steps
    direction = moment_new / first_fix / (jnp.sqrt(square_new / second_fix) + adam_eps)
    if decayed:
        direction = direction + decay_rate * weight
    return (weight - learn_rate * direction, moment_new, square_new)


def dot_on(left, right, left_dim, right_dim):
    return lax.dot_general(
        left, right, (((left_dim,), (right_dim,)), ((), ())), preferred_element_type=jnp.float32
    )


def head_probs(query_t, key_t, allowed):
    scores = dot_on(query_t, key_t, 0, 0) * HD ** (-0.5)
    scores = jnp.where(allowed, scores, masked_score)
    row_max = jnp.max(scores, axis=1, keepdims=True)
    weights = jnp.exp(scores - row_max)
    return weights / jnp.sum(weights, axis=1, keepdims=True)


def forward_kernel(query_pos, key_pos, query_ref, key_ref, value_ref, out_ref):
    allowed = query_pos[...] >= key_pos[...]
    probs = head_probs(query_ref[...], key_ref[...], allowed).astype(jnp.bfloat16)
    out_ref[...] = dot_on(value_ref[...], probs, 1, 1).astype(jnp.bfloat16)


def backward_kernel(
    query_pos, key_pos, query_ref, key_ref, value_ref, out_ref, dout_ref, dquery, dkey, dvalue
):
    allowed = query_pos[...] >= key_pos[...]
    query_t = query_ref[...]
    key_t = key_ref[...]
    dout_t = dout_ref[...]
    probs = head_probs(query_t, key_t, allowed)
    dprobs = dot_on(dout_t, value_ref[...], 0, 0)
    products = dout_t.astype(jnp.float32) * out_ref[...].astype(jnp.float32)
    delta = jnp.sum(products.T, axis=1, keepdims=True)
    dscores = (probs * (dprobs - delta) * HD ** (-0.5)).astype(jnp.bfloat16)
    dquery[...] = dot_on(key_t, dscores, 1, 1).astype(jnp.bfloat16)
    dkey[...] = dot_on(query_t, dscores, 1, 0).astype(jnp.bfloat16)
    dvalue[...] = dot_on(dout_t, probs.astype(jnp.bfloat16), 1, 0).astype(jnp.bfloat16)


def attention(kernel, query_pos, key_pos, features, out_rows):
    queries, keys = query_pos.shape[0], key_pos.shape[1]
    whole = lambda array: pl.BlockSpec(array.shape, lambda h: (0, 0))
    block = lambda width: pl.BlockSpec((HD, width), lambda h: (h, 0))
    shapes = [jax.ShapeDtypeStruct((H * HD, width), jnp.bfloat16) for width in out_rows]
    flops = 2 * H * HD * queries * keys * (2 if len(out_rows) == 1 else 5)
    return pl.pallas_call(
        kernel,
        grid=(H,),
        in_specs=[whole(query_pos), whole(key_pos)] + [block(x.shape[1]) for x in features],
        out_specs=[block(width) for width in out_rows],
        out_shape=shapes,
        cost_estimate=pl.CostEstimate(
            flops=flops, bytes_accessed=8 * H * HD * keys, transcendentals=H * queries * keys
        ),
    )(query_pos, key_pos, *features)


def exchange(blocks):
    return lax.all_to_all(blocks, "ctx", split_axis=0, concat_axis=0, tiled=True)


def scatter_rows(partial):
    return lax.psum_scatter(
        partial.astype(jnp.bfloat16), "ctx", scatter_dimension=0, tiled=True
    ).astype(jnp.float32)


def gather_rows(rows):
    return lax.all_gather(rows, "ctx", axis=0, tiled=True)


def local(
    inputs,
    out_grad,
    pair_blocks,
    triple_weight,
    merge_weight,
    expand_weight,
    shrink_weight,
    vector_params,
    triple_moment,
    merge_moment,
    expand_moment,
    shrink_moment,
    vector_moment,
    triple_square,
    merge_square,
    expand_square,
    shrink_square,
    vector_square,
):
    bf16 = jnp.bfloat16
    n = lax.axis_size("ctx")
    m = lax.axis_size("dp")
    here = lax.axis_index("ctx")
    rows = inputs.shape[1]
    total = rows * n
    feat = D // n
    hidden_width = m * expand_weight.shape[1]
    wide = hidden_width // n
    stream = inputs[0]
    cotangent = out_grad[0]
    offsets = jnp.arange(BLK, dtype=jnp.int32)
    positions = (pair_blocks.reshape(-1)[:, None] * BLK + offsets[None, :]).reshape(-1)
    query_pos = lax.dynamic_slice_in_dim(positions, here * rows, rows)[:, None]
    key_pos = positions[None, :]

    packed = jnp.concatenate(
        [
            triple_weight.astype(bf16),
            merge_weight.astype(bf16),
            expand_weight.astype(bf16),
            vector_params.astype(bf16),
        ],
        axis=1,
    )
    normed_one, inverse_one = layer_norm(stream)
    tw, mw, ew = triple_weight.shape[1], merge_weight.shape[1], expand_weight.shape[1]
    columns = lax.all_gather(packed, "dp", axis=0)

    def take(start, width):
        return columns[:, :, start : start + width].transpose(1, 0, 2).reshape(feat, m * width)

    triple_rows = take(0, tw)
    merge_rows = take(tw, mw)
    expand_rows = take(tw + mw, ew)
    vector_rows = take(tw + mw + ew, vector_params.shape[1])
    normed_send, columns_done = lax.optimization_barrier((normed_one.astype(bf16), columns))
    normed_full = gather_rows(normed_send)
    vector_rows, normed_full = lax.optimization_barrier((vector_rows, normed_full))
    vectors = gather_rows(vector_rows).astype(jnp.float32)
    shrink_send, vectors = lax.optimization_barrier((shrink_weight.astype(bf16), vectors))
    w_shrink = lax.all_gather(shrink_send, "dp", axis=0).transpose(1, 0, 2).reshape(wide, D)
    send = jnp.concatenate(
        [
            triple_rows.reshape(feat, 3, n, feat).transpose(2, 0, 1, 3).reshape(n, feat, 3 * feat),
            expand_rows.reshape(feat, n, wide).transpose(1, 0, 2),
        ],
        axis=2,
    )
    got = exchange(send).reshape(D, 3 * feat + wide)
    w_triple = got[:, : 3 * feat]
    w_expand = got[:, 3 * feat :]
    gain_one = vectors[:, 0]
    shift_one = vectors[:, 1]
    query_bias = lax.dynamic_slice_in_dim(vectors[:, 2], here * feat, feat)
    value_bias = lax.dynamic_slice_in_dim(vectors[:, 3], here * feat, feat)
    merge_bias = vectors[:, 4]
    gain_two = vectors[:, 5]
    shift_two = vectors[:, 6]
    shrink_bias = vectors[:, 7]
    expand_bias = lax.dynamic_slice_in_dim(vectors[:, 8:].T.reshape(-1), here * wide, wide)

    act_one = (normed_full.astype(jnp.float32) * gain_one + shift_one).astype(bf16)
    bias = jnp.concatenate([query_bias, jnp.zeros_like(query_bias), value_bias])
    triple_t = (dot_on(w_triple, act_one, 0, 1) + bias[:, None]).astype(bf16)
    query_t = exchange(triple_t[:feat].reshape(feat, n, rows).transpose(1, 0, 2)).reshape(D, rows)
    pair_send, w_shrink = lax.optimization_barrier(
        (triple_t[feat:].reshape(2, feat, total), w_shrink)
    )
    both = lax.all_gather(pair_send, "ctx", axis=0)
    merge_rows, both = lax.optimization_barrier((merge_rows, both))
    w_merge = gather_rows(merge_rows)
    key_t = both[:, 0].reshape(D, total)
    value_t = both[:, 1].reshape(D, total)
    (attended_t,) = attention(
        forward_kernel, query_pos, key_pos, (query_t, key_t, value_t), (rows,)
    )
    middle = stream + dot_on(attended_t, w_merge, 0, 0) + merge_bias
    normed_two, inverse_two = layer_norm(middle)
    act_two = gather_rows((normed_two * gain_two + shift_two).astype(bf16))
    cot_send, act_two = lax.optimization_barrier((cotangent.astype(bf16), act_two))
    cot_full = gather_rows(cot_send)
    pre_act = dot_on(act_two, w_expand, 1, 0) + expand_bias
    hidden_b = gelu_value(pre_act).astype(bf16)
    dpre = dot_on(cot_full, w_shrink, 1, 1) * gelu_slope(pre_act)
    dpre_b = dpre.astype(bf16)
    expand_bias_grad = jnp.sum(dpre, axis=0)
    dact_two = scatter_rows(dot_on(dpre_b, w_expand, 1, 1))
    out_part = dot_on(hidden_b, w_shrink, 1, 0).astype(bf16)
    out_part, dact_two = lax.optimization_barrier((out_part, dact_two))
    block_rows = scatter_rows(out_part)
    block_out = middle + block_rows + shrink_bias
    shrink_part = dot_on(hidden_b, cot_full, 0, 0).astype(bf16)
    expand_part = dot_on(act_two, dpre_b, 0, 0).astype(bf16)
    shrink_bias_grad = jnp.sum(cotangent, axis=0)
    gain_two_grad = jnp.sum(dact_two * normed_two, axis=0)
    shift_two_grad = jnp.sum(dact_two, axis=0)
    dmiddle = cotangent + norm_back(dact_two, normed_two, inverse_two, gain_two)
    dmiddle_b = dmiddle.astype(bf16)
    merge_part = dot_on(attended_t, dmiddle_b, 1, 0).astype(bf16)
    merge_bias_grad = jnp.sum(dmiddle, axis=0)
    dattended_t = dot_on(w_merge, dmiddle_b, 1, 1).astype(bf16)
    dquery_t, dkey_t, dvalue_t = attention(
        backward_kernel,
        query_pos,
        key_pos,
        (query_t, key_t, value_t, attended_t, dattended_t),
        (rows, total, total),
    )
    dquery_c = exchange(dquery_t.reshape(n, feat, rows)).transpose(1, 0, 2).reshape(feat, total)
    dkey_c = lax.psum_scatter(dkey_t, "ctx", scatter_dimension=0, tiled=True)
    dvalue_c = lax.psum_scatter(dvalue_t, "ctx", scatter_dimension=0, tiled=True)
    dtriple_t = jnp.concatenate([dquery_c, dkey_c, dvalue_c], axis=0)
    query_bias_grad = jnp.sum(dquery_c.astype(jnp.float32), axis=1)
    value_bias_grad = jnp.sum(dvalue_c.astype(jnp.float32), axis=1)
    dact_one = scatter_rows(dot_on(dtriple_t, w_triple, 0, 1))
    triple_part = dot_on(act_one, dtriple_t, 0, 1).astype(bf16)
    shrink_part, expand_part, merge_part, triple_part, dact_one = lax.optimization_barrier(
        (shrink_part, expand_part, merge_part, triple_part, dact_one)
    )
    gain_one_grad = jnp.sum(dact_one * normed_one, axis=0)
    shift_one_grad = jnp.sum(dact_one, axis=0)
    input_rows = dmiddle + norm_back(dact_one, normed_one, inverse_one, gain_one)

    def place(piece, size):
        return lax.dynamic_update_slice_in_dim(
            jnp.zeros((size,), jnp.float32), piece, here * piece.shape[0], 0
        )

    vector_local = jnp.concatenate(
        [
            jnp.stack(
                [
                    gain_one_grad,
                    shift_one_grad,
                    place(query_bias_grad, D),
                    place(value_bias_grad, D),
                    merge_bias_grad,
                    gain_two_grad,
                    shift_two_grad,
                    shrink_bias_grad,
                ],
                axis=1,
            ),
            place(expand_bias_grad, hidden_width).reshape(-1, D).T,
        ],
        axis=1,
    )
    vector_part = lax.psum_scatter(vector_local, "ctx", scatter_dimension=0, tiled=True)
    vector_grad = lax.psum_scatter(vector_part, "dp", scatter_dimension=1, tiled=True)

    def own_block(part, groups, width):
        pieces = part.reshape(n, feat, groups, -1)
        if feat % m:
            spread = exchange(pieces).transpose(1, 2, 0, 3).reshape(feat, m, width)
            return lax.psum_scatter(spread.transpose(1, 0, 2), "dp", scatter_dimension=0)
        fine = feat // m
        split = pieces.reshape(n, m, fine, groups, -1).transpose(1, 0, 2, 3, 4)
        split = split.reshape(m, n, fine, -1)
        summed = lax.psum_scatter(split, "dp", scatter_dimension=0)
        spread = exchange(summed).reshape(n, fine, groups, -1).transpose(1, 2, 0, 3)
        spread = spread.reshape(fine, m, width).transpose(1, 0, 2)
        return lax.all_to_all(spread, "dp", split_axis=0, concat_axis=0, tiled=True).reshape(
            feat, width
        )

    def sum_columns(part):
        pieces = part.reshape(part.shape[0], m, -1).transpose(1, 0, 2)
        return lax.psum_scatter(pieces, "dp", scatter_dimension=0)

    shrink_grad = sum_columns(shrink_part).astype(jnp.float32)
    merge_grad = lax.psum_scatter(
        sum_columns(merge_part), "ctx", scatter_dimension=0, tiled=True
    ).astype(jnp.float32)
    expand_grad = own_block(expand_part, 1, ew).astype(jnp.float32)
    triple_grad = own_block(triple_part, 3, tw).astype(jnp.float32)
    triple_new, triple_moment_new, triple_square_new = adam_update(
        triple_weight, triple_grad, triple_moment, triple_square, True
    )
    merge_new, merge_moment_new, merge_square_new = adam_update(
        merge_weight, merge_grad, merge_moment, merge_square, True
    )
    expand_new, expand_moment_new, expand_square_new = adam_update(
        expand_weight, expand_grad, expand_moment, expand_square, True
    )
    shrink_new, shrink_moment_new, shrink_square_new = adam_update(
        shrink_weight, shrink_grad, shrink_moment, shrink_square, True
    )
    vector_new, vector_moment_new, vector_square_new = adam_update(
        vector_params, vector_grad, vector_moment, vector_square, False
    )
    return (
        block_out[None],
        input_rows[None],
        triple_grad,
        merge_grad,
        expand_grad,
        shrink_grad,
        vector_grad,
        triple_new,
        merge_new,
        expand_new,
        shrink_new,
        vector_new,
        triple_moment_new,
        merge_moment_new,
        expand_moment_new,
        shrink_moment_new,
        vector_moment_new,
        triple_square_new,
        merge_square_new,
        expand_square_new,
        shrink_square_new,
        vector_square_new,
    )


def solution(mesh):
    in_specs = (
        P("dp", "ctx", None),
        P("dp", "ctx", None),
        P(),
        P("ctx", "dp"),
        P("ctx", "dp"),
        P("ctx", "dp"),
        P("ctx", "dp"),
        P("ctx", "dp"),
        P("ctx", "dp"),
        P("ctx", "dp"),
        P("ctx", "dp"),
        P("ctx", "dp"),
        P("ctx", "dp"),
        P("ctx", "dp"),
        P("ctx", "dp"),
        P("ctx", "dp"),
        P("ctx", "dp"),
        P("ctx", "dp"),
    )
    out_specs = (
        P("dp", "ctx", None),
        P("dp", "ctx", None),
        P("ctx", "dp"),
        P("ctx", "dp"),
        P("ctx", "dp"),
        P("ctx", "dp"),
        P("ctx", "dp"),
        P("ctx", "dp"),
        P("ctx", "dp"),
        P("ctx", "dp"),
        P("ctx", "dp"),
        P("ctx", "dp"),
        P("ctx", "dp"),
        P("ctx", "dp"),
        P("ctx", "dp"),
        P("ctx", "dp"),
        P("ctx", "dp"),
        P("ctx", "dp"),
        P("ctx", "dp"),
        P("ctx", "dp"),
        P("ctx", "dp"),
        P("ctx", "dp"),
    )
    return jax.shard_map(local, mesh=mesh, in_specs=in_specs, out_specs=out_specs, check_vma=False)
```
